32 devices in a mesh: ctx: 8 (over z, x), head: 4 (over y, core).
Axes of the slice: x: 2, y: 2, z: 4, core: 2. Of those that a mesh axis runs over, the one named last changes fastest.
Arguments:
- queries: bfloat16 [8192, 4096], P('ctx', 'head'), may hold values from -6 to 6
- key_vectors: bfloat16 [8192, 4096], P('ctx', 'head'), may hold values from -6 to 6
- value_vectors: bfloat16 [8192, 4096], P('ctx', 'head'), may hold values from -6 to 6
- level_weights: float32 [4, 32, 8192], P(None, 'head', 'ctx'), may hold values from 0.2 to 2
- out_grad: bfloat16 [8192, 4096], P('ctx', 'head'), may hold values from -0.109375 to 0.109375
Outputs:
- attn_out: bfloat16 [8192, 4096], P('ctx', 'head')
- weight_grad: float32 [4096, 4096], P('ctx', 'head')
The draws below stay inside these ranges and needn't reach their ends.
All inputs are finite; a program needn't handle non-finite values.
Results may differ from the reference program's by a relative error of at most 0.005.
Values may be sent and summed in bfloat16 or wider, within the bound.
No kernel may reach another device: no remote copies, remote signals or barrier semaphores. Data moves between devices by JAX's collectives and lax.ppermute only.
A program may use at most 64 MiB of HBM per device.

```python
import math
import jax
import jax.numpy as jnp
from jax import lax

MODEL_DIM = 4096
HEADS = 32
HEAD_DIM = 128
GROUP = 1024
TOKENS = 8192
LEVELS = 4


def raised(result, stream_key, source, target, shards_of, factor):
    def block_of(position):
        return (jnp.arange(result.shape[position]) // (result.shape[position] // shards_of)).reshape((-1,) + (1,) * (result.ndim - 1 - position))

    near = jax.random.permutation(stream_key, shards_of)[block_of(target)]
    far = (block_of(target) + shards_of // 2) % shards_of
    return jnp.where((block_of(source) == near) | (block_of(source) == far), factor * result, result)


def block_levels(own_key, shape, shards, smallest, high):
    def one(dim, parts):
        draws = jax.random.uniform(jax.random.fold_in(jax.random.fold_in(own_key, 6), dim), (parts,), jnp.float32, smallest / len(shards), high / len(shards))
        return jnp.repeat(jnp.exp(draws), shape[dim] // parts).reshape((-1,) + (1,) * (len(shape) - dim - 1))

    loudness = one(*shards[0])
    for cut in shards[1:]:
        loudness = loudness * one(*cut)
    return loudness


def scatter_about(key, extent, deviation, limit, cuts=(), held_as=jnp.bfloat16):
    factor_of = block_levels(key, extent, cuts, -0.22, 0.18) if cuts else 1.0
    entries = jax.random.normal(key, extent, jnp.float32) * deviation * factor_of
    return jnp.minimum(jnp.maximum(entries, -limit), limit).astype(held_as)


def bell_draw_with(key, shape, width, reach, shards, heavy, held_as=jnp.bfloat16):
    entries = width * jax.random.normal(key, shape, jnp.float32)
    if shards:
        entries = entries * block_levels(key, shape, shards, -0.22, 0.18)
    return jnp.clip(raised(entries, jax.random.fold_in(key, 3), *heavy), -reach, reach).astype(held_as)


def setup_inputs(seed: int = 0) -> dict:
    splits = jax.random.split(jax.random.key(seed), 6)
    return {
        "queries": scatter_about(splits[0], (TOKENS, HEADS * HEAD_DIM), 1.0, 6.0, ((0, 8), (1, 4))),
        "key_vectors": scatter_about(splits[1], (TOKENS, HEADS * HEAD_DIM), 1.0, 6.0, ((0, 8), (1, 4))),
        "value_vectors": scatter_about(splits[2], (TOKENS, HEADS * HEAD_DIM), 1.0, 6.0, ((0, 8), (1, 4))),
        "level_weights": jnp.clip(jnp.exp(math.log(2.0) - 2.3025851 * jax.random.uniform(splits[3], (LEVELS, HEADS, TOKENS), jnp.float32) ** block_levels(splits[3], (LEVELS, HEADS, TOKENS), ((1, 4), (2, 8)), -0.2, 0.2)), 0.2, 2.0),
        "out_grad": bell_draw_with(splits[4], (TOKENS, MODEL_DIM), 0.005, 0.109375, ((0, 8), (1, 4)), (0, 1, 8, 2.0)),
    }


def reference(queries, key_vectors, value_vectors, level_weights, out_grad):
    group_count = TOKENS // GROUP
    query_heads = queries.reshape(group_count, GROUP, HEADS, HEAD_DIM)
    key_heads = key_vectors.reshape(group_count, GROUP, HEADS, HEAD_DIM)
    value_heads = value_vectors.reshape(group_count, GROUP, HEADS, HEAD_DIM)
    per_level = level_weights.reshape(LEVELS, HEADS, group_count, GROUP).transpose(0, 2, 3, 1)[..., None]

    def intra(inputs):
        query_group, key_group, value_group = inputs
        scores = jnp.einsum('thd,shd->hts', query_group.astype(jnp.float32), key_group.astype(jnp.float32)) * (HEAD_DIM * GROUP) ** -0.5
        causal = jnp.arange(GROUP)[:, None] >= jnp.arange(GROUP)[None, :]
        weights = jnp.where(causal[None], scores, 0.0).astype(jnp.bfloat16)
        return jnp.einsum('hts,she->the', weights.astype(jnp.float32), value_group.astype(jnp.float32))

    local_part = lax.map(intra, (query_heads, key_heads, value_heads))
    combined = per_level[0] * local_part
    own_state = jnp.einsum('nshd,nshe->nhde', key_heads.astype(jnp.float32), value_heads.astype(jnp.float32))
    group_ids = jnp.arange(group_count, dtype=jnp.int32)
    for level in range(LEVELS - 1):
        block_sums = own_state.reshape(group_count >> level, 2 ** level, HEADS, HEAD_DIM, HEAD_DIM).sum(axis=1)
        previous = jnp.maximum((group_ids >> level) - 1, 0).astype(jnp.int32)
        is_upper = ((group_ids >> level) & 1).astype(jnp.float32)
        bucket = block_sums[previous] * is_upper[:, None, None, None]
        bucket_bf = bucket.astype(jnp.bfloat16)
        state_read = jnp.einsum('nthd,nhde->nthe', query_heads.astype(jnp.float32), bucket_bf.astype(jnp.float32))
        combined = combined + per_level[level + 1] * ((HEAD_DIM * GROUP * 2 ** level) ** -0.5) * state_read
    attn_out = combined.reshape(TOKENS, HEADS * HEAD_DIM).astype(jnp.bfloat16)
    weight_grad = jnp.dot(out_grad.T, attn_out, preferred_element_type=jnp.float32)
    return attn_out, weight_grad
```

```python
import functools

import jax
import jax.numpy as jnp
from jax import lax
from jax.experimental import pallas as pl
from jax.experimental.pallas import tpu as pltpu
from jax.sharding import PartitionSpec as P

HEAD_DIM = 128


def swapped(shard, axis, bit):
    return lax.ppermute(shard, axis, [(i, i ^ 1 << bit) for i in range(lax.axis_size(axis))])


def contract_rows(a, b):
    return lax.dot_general(a, b, (((0,), (0,)), ((), ())), preferred_element_type=jnp.float32)


def state_kernel(k_ref, v_ref, own_ref, own_bf_ref):
    own = contract_rows(k_ref[...], v_ref[...])
    own_ref[0] = own
    own_bf_ref[0] = own.astype(jnp.bfloat16)


def own_states(keys, values):
    length, columns = keys.shape
    heads = columns // HEAD_DIM
    column = pl.BlockSpec((length, HEAD_DIM), lambda h: (0, h))
    square = pl.BlockSpec((1, HEAD_DIM, HEAD_DIM), lambda h: (h, 0, 0))
    return pl.pallas_call(
        state_kernel,
        grid=(heads,),
        in_specs=[column, column],
        out_specs=[square, square],
        out_shape=[
            jax.ShapeDtypeStruct((heads, HEAD_DIM, HEAD_DIM), jnp.float32),
            jax.ShapeDtypeStruct((heads, HEAD_DIM, HEAD_DIM), jnp.bfloat16),
        ],
        cost_estimate=pl.CostEstimate(
            flops=2 * length * columns * HEAD_DIM, bytes_accessed=4 * length * columns, transcendentals=0
        ),
        name="own_states",
    )(keys, values)


def near_kernel(scale, part, q_ref, k_ref, v_ref, near_ref):
    length = q_ref.shape[0]
    causal = lax.broadcasted_iota(jnp.int32, (part, part), 0) >= lax.broadcasted_iota(jnp.int32, (part, part), 1)
    state = jnp.zeros((HEAD_DIM, HEAD_DIM), jnp.float32)
    for first in range(0, length, part):
        rows = slice(first, first + part)
        q, k, v = q_ref[rows], k_ref[rows], v_ref[rows]
        scores = lax.dot_general(q, k, (((1,), (1,)), ((), ())), preferred_element_type=jnp.float32) * scale
        weights = jnp.where(causal, scores, 0.0).astype(jnp.bfloat16)
        near = jnp.dot(weights, v, preferred_element_type=jnp.float32)
        if first:
            near = near + jnp.dot(q, state.astype(jnp.bfloat16), preferred_element_type=jnp.float32) * scale
        near_ref[rows] = near
        if first + part < length:
            state = state + contract_rows(k, v)


def near_parts(queries, keys, values):
    length, columns = keys.shape
    heads = columns // HEAD_DIM
    part = min(256, length)
    column = pl.BlockSpec((length, HEAD_DIM), lambda h: (0, h))
    return pl.pallas_call(
        functools.partial(near_kernel, (HEAD_DIM * length) ** -0.5, part),
        grid=(heads,),
        in_specs=[column, column, column],
        out_specs=column,
        out_shape=jax.ShapeDtypeStruct((length, columns), jnp.float32),
        cost_estimate=pl.CostEstimate(
            flops=4 * length * columns * (part + HEAD_DIM), bytes_accessed=10 * length * columns, transcendentals=0
        ),
        name="near_parts",
    )(queries, keys, values)


def combine_kernel(levels, factor_ref, q_ref, near_ref, weight_ref, bucket_ref, *refs):
    chunk_ref, full_ref = refs[-2:]
    weights = jnp.transpose(weight_ref[0], (1, 0))
    combined = weights[:, 0:1] * near_ref[...]
    q = q_ref[...]
    for level in range(levels):
        read = jnp.dot(q, bucket_ref[level, 0], preferred_element_type=jnp.float32)
        combined = combined + (weights[:, level + 1 : level + 2] * factor_ref[level]) * read
    out = combined.astype(jnp.bfloat16)
    chunk_ref[...] = out
    full_ref[...] = out


def combine(first, factors, queries, near, weights, buckets, full):
    length, columns = queries.shape
    levels, heads = buckets.shape[0], buckets.shape[1]
    column = pl.BlockSpec((length, HEAD_DIM), lambda h: (0, first + h))
    in_specs = [
        pl.BlockSpec(memory_space=pltpu.SMEM),
        column,
        column,
        pl.BlockSpec((1, levels + 1, length), lambda h: (first + h, 0, 0)),
        pl.BlockSpec((levels, 1, HEAD_DIM, HEAD_DIM), lambda h: (0, h, 0, 0)),
    ]
    operands = [factors, queries, near, weights, buckets]
    aliases = {}
    if full is not None:
        in_specs.append(pl.BlockSpec(memory_space=pl.ANY))
        operands.append(full)
        aliases = {5: 1}
    return pl.pallas_call(
        functools.partial(combine_kernel, levels),
        grid=(heads,),
        in_specs=in_specs,
        out_specs=[pl.BlockSpec((length, HEAD_DIM), lambda h: (0, h)), column],
        out_shape=[
            jax.ShapeDtypeStruct((length, heads * HEAD_DIM), jnp.bfloat16),
            jax.ShapeDtypeStruct((length, columns), jnp.bfloat16),
        ],
        input_output_aliases=aliases,
        cost_estimate=pl.CostEstimate(
            flops=2 * length * heads * HEAD_DIM * HEAD_DIM * levels,
            bytes_accessed=10 * length * heads * HEAD_DIM,
            transcendentals=0,
        ),
        name="combine",
    )(*operands)


def grad_kernel(count, groups, place_ref, *refs):
    blocks, attns, (send_ref, keep_ref) = refs[: 2 * count], refs[2 * count : -2], refs[-2:]
    half, rows = send_ref.shape[0], send_ref.shape[1]
    for k in range(count):
        total = jnp.dot(blocks[2 * k][...], attns[0][...], preferred_element_type=jnp.float32)
        total = total + jnp.dot(blocks[2 * k + 1][...], attns[1][...], preferred_element_type=jnp.float32)
        for i in range(groups):
            place = place_ref[k * groups + i]
            part = total[i * rows : (i + 1) * rows]

            @pl.when(place >= half)
            def _(place=place, part=part):
                send_ref[place - half] = part.astype(jnp.bfloat16)

            @pl.when(place < half)
            def _(place=place, part=part):
                keep_ref[place] = part


def grad_parts(places, blocks, own, other, rows):
    count = len(blocks) // 2
    groups = blocks[0].shape[0] // rows
    half = count * groups // 2
    columns = own.shape[1]
    whole = pl.BlockSpec(memory_space=pltpu.VMEM)
    return pl.pallas_call(
        functools.partial(grad_kernel, count, groups),
        in_specs=[pl.BlockSpec(memory_space=pltpu.SMEM)] + [whole] * (len(blocks) + 2),
        out_specs=[whole, whole],
        out_shape=[
            jax.ShapeDtypeStruct((half, rows, columns), jnp.bfloat16),
            jax.ShapeDtypeStruct((half, rows, columns), jnp.float32),
        ],
        cost_estimate=pl.CostEstimate(
            flops=2 * sum(b.size for b in blocks) * columns,
            bytes_accessed=2 * sum(b.size for b in blocks) + 4 * own.size + 6 * half * rows * columns,
            transcendentals=0,
        ),
        name="grad_parts",
    )(places, *blocks, own, other)


def reversed_bits(value, bits):
    out = jnp.zeros_like(value)
    for bit in range(bits):
        out = out | ((value >> bit & 1) << (bits - 1 - bit))
    return out


def chunk_sizes(heads):
    sizes = [1]
    while sum(sizes) < heads:
        left = heads - sum(sizes)
        sizes.append(2 if left > 2 else 1)
    return sizes


def body(queries, key_vectors, value_vectors, level_weights, out_grad):
    length, columns = queries.shape
    heads = columns // HEAD_DIM
    levels = level_weights.shape[0] - 1
    n_ctx, n_head = lax.axis_size("ctx"), lax.axis_size("head")
    ctx_bits, head_bits = n_ctx.bit_length() - 1, n_head.bit_length() - 1
    ctx, head = lax.axis_index("ctx"), lax.axis_index("head")
    rows = out_grad.shape[1] * n_head // n_ctx
    groups = n_ctx // n_head // 2
    sizes = chunk_sizes(heads)

    own, own_bf = own_states(key_vectors, value_vectors)
    spans, first = [], 0
    for size in (1, heads - 1):
        spans.append((first, first + size))
        first += size
    bucket_spans = []
    for begin, end in spans:
        total, sent, received = own[begin:end], own_bf[begin:end], []
        for level in range(levels):
            partner = swapped(sent, "ctx", level)
            received.append(partner)
            if level + 1 < levels:
                total = total + partner.astype(jnp.float32)
                sent = total.astype(jnp.bfloat16)
        bucket_spans.append(jnp.stack(received))
    upper = (ctx >> jnp.arange(levels) & 1).astype(jnp.float32)
    factors = upper * jnp.array([(HEAD_DIM * length * 2.0**level) ** (-0.5) for level in range(levels)], jnp.float32)

    grad_rows = jnp.transpose(out_grad).reshape(groups, 2, rows, length)
    low, high = grad_rows[:, 0], grad_rows[:, 1]
    bit = ctx & 1
    kept = jnp.where(bit == 0, low, high).reshape(groups * rows, length)
    given = jnp.where(bit == 0, high, low).reshape(groups * rows, length)
    pair = {0: (kept, swapped(given, "ctx", 0))}
    for head_bit in reversed(range(head_bits)):
        for k in list(pair):
            pair[k | 1 << head_bit] = tuple(swapped(part, "head", head_bit) for part in pair[k])
    blocks = [part for k in range(n_head) for part in pair[k]]
    order = jnp.arange(n_head)[:, None] ^ head
    index = (order * groups + jnp.arange(groups)[None, :]).reshape(-1) ^ (ctx >> 1)
    places = reversed_bits(index, ctx_bits - 1).astype(jnp.int32)

    near = near_parts(queries, key_vectors, value_vectors)
    weights = jnp.transpose(level_weights, (1, 0, 2))
    full, results, first = None, [], 0
    for number, size in enumerate(sizes):
        span = 0 if number == 0 else 1
        offset = first - spans[span][0]
        buckets = bucket_spans[span][:, offset : offset + size]
        chunk, full = combine(first, factors, queries, near, weights, buckets, full)
        other = swapped(chunk, "ctx", 0)
        send, keep = grad_parts(places, blocks, chunk, other, rows)
        for step in range(1, ctx_bits):
            keep = keep + swapped(send, "ctx", step).astype(jnp.float32)
            if step + 1 < ctx_bits:
                half = keep.shape[0] // 2
                send = keep[half:].astype(jnp.bfloat16)
                keep = keep[:half]
        results.append(keep[0])
        first += size
    return full, jnp.concatenate(results, axis=1)


def solution(mesh):
    return jax.shard_map(
        body,
        mesh=mesh,
        in_specs=(
            P("ctx", "head"),
            P("ctx", "head"),
            P("ctx", "head"),
            P(None, "head", "ctx"),
            P("ctx", "head"),
        ),
        out_specs=(P("ctx", "head"), P("ctx", "head")),
        check_vma=False,
    )
```
